32 devices in a mesh: row: 4 (over y, x), col: 8 (over z, core).
Axes of the slice: x: 2, y: 2, z: 4, core: 2. Of those that a mesh axis runs over, the one named last changes fastest.
Arguments:
- panel_factor: bfloat16 [128, 20480], P('row', 'col'), may hold values from -0.5 to 0.5
- diag_inverse: bfloat16 [128, 128], P('col'), may hold values from -0.5 to 0.5
- panel_rhs: bfloat16 [128, 18432], P('col', 'row'), may hold values from -6 to 6
- trail_rhs: bfloat16 [18432, 20480], P('row', 'col'), may hold values from -6 to 6
- forward_field: bfloat16 [18432, 20480], P('row', 'col'), may hold values from -6 to 6
- pivot: int32 [128], replicated, may hold values from 0 to 127, each once
- panel_harmonic: int32 [2, 128], replicated, may hold values from 0 to 90
- trail_harmonic: int32 [2, 20480], P(None, 'col'), may hold values from 0 to 90
Outputs:
- panel_adjoint: bfloat16 [128, 18432], P(None, 'row')
- trail_update: bfloat16 [18432, 20480], P('row', 'col')
- eps_grad: float32 [36864], P(('row', 'col'))
The draws below stay inside these ranges and needn't reach their ends.
All inputs are finite; a program needn't handle non-finite values.
Results may differ from the reference program's by a relative error of at most 0.0039.
Values may be sent and summed in bfloat16 or wider, within the bound.
No kernel may reach another device: no remote copies, remote signals or barrier semaphores. Data moves between devices by JAX's collectives and lax.ppermute only.
A program may use at most 128 MiB of HBM per device.

```python
import math
import jax
import jax.numpy as jnp
from jax import lax

NB = 128
NT = 20480
S = 18432
ORDERS = 91
DPITCH = 192
NDIAG = 36864


def set_ends(result, rng, least, largest):
    index_at = [jax.random.randint(jax.random.fold_in(rng, axis), (), 0, length) for axis, length in enumerate(result.shape)]
    longest = result.shape.index(max(result.shape))
    next_to = index_at[:longest] + [(index_at[longest] + 1) % result.shape[longest]] + index_at[longest + 1:]
    return result.at[tuple(index_at)].set(least).at[tuple(next_to)].set(largest)


def shard_levels(rng, extent, shards, least, largest):
    def one(axis_at, shards_of):
        draws = jax.random.uniform(jax.random.fold_in(jax.random.fold_in(rng, 6), axis_at), (shards_of,), jnp.float32, least / len(shards), largest / len(shards))
        return jnp.repeat(jnp.exp(draws), extent[axis_at] // shards_of).reshape((-1,) + (1,) * (len(extent) - axis_at - 1))

    factor_of = one(*shards[0])
    for cut in shards[1:]:
        factor_of = factor_of * one(*cut)
    return factor_of


def centred(rng, dims, deviation, most, split=(), kind=jnp.bfloat16):
    entries = jax.random.normal(rng, dims, jnp.float32) * deviation
    if len(split) > 0:
        entries = shard_levels(rng, dims, split, -0.22, 0.18) * entries
    return jnp.clip(entries, min=-most, max=most).astype(kind)


def setup_inputs(seed: int = 0) -> dict:
    keys = jax.random.split(jax.random.key(seed), 9)
    panel_factor = centred(keys[0], (NB, NT), NB ** -0.5, 0.5, ((0, 4), (1, 8)))
    diag_inverse = centred(keys[1], (NB, NB), NB ** -0.5, 0.5, ((0, 8),))
    panel_rhs = centred(keys[2], (NB, S), 1.0, 6.0, ((0, 8), (1, 4)))
    trail_rhs = centred(keys[3], (S, NT), 1.0, 6.0, ((0, 4), (1, 8)))
    forward_field = centred(keys[4], (S, NT), 1.0, 6.0, ((0, 4), (1, 8)))
    pivot = jax.random.permutation(keys[5], NB).astype(jnp.int32)
    panel_harmonic = set_ends(jax.random.randint(keys[6], (2, NB), 0, ORDERS), jax.random.fold_in(keys[6], 1), 0, ORDERS - 1).astype(jnp.int32)
    trail_harmonic = set_ends(jax.random.randint(keys[7], (2, NT), 0, ORDERS), jax.random.fold_in(keys[7], 1), 0, ORDERS - 1).astype(jnp.int32)
    return dict(panel_factor=panel_factor, diag_inverse=diag_inverse, panel_rhs=panel_rhs, trail_rhs=trail_rhs, forward_field=forward_field, pivot=pivot, panel_harmonic=panel_harmonic, trail_harmonic=trail_harmonic)


def reference(panel_factor, diag_inverse, panel_rhs, trail_rhs, forward_field, pivot, panel_harmonic, trail_harmonic):
    panel_adjoint = jnp.dot(diag_inverse.T, panel_rhs, preferred_element_type=jnp.float32).astype(jnp.bfloat16)
    blocks = 16
    block_size = S // blocks
    trail_blocks = trail_rhs.reshape(blocks, block_size, NT)
    field_blocks = forward_field.reshape(blocks, block_size, NT)
    adjoint_blocks = panel_adjoint.reshape(NB, blocks, block_size).transpose(1, 0, 2)

    def accumulate(correlation, inputs):
        adjoint_piece, trail_piece, field_piece = inputs
        update = jnp.dot(adjoint_piece.T, panel_factor, preferred_element_type=jnp.float32)
        fresh = (trail_piece.astype(jnp.float32) - update).astype(jnp.bfloat16)
        correlation = correlation + jnp.dot(adjoint_piece, field_piece, preferred_element_type=jnp.float32)
        return (correlation, fresh)
    initial = jnp.zeros((NB, NT), jnp.float32)
    correlation, fresh_blocks = lax.scan(accumulate, initial, (adjoint_blocks, trail_blocks, field_blocks))
    trail_update = fresh_blocks.reshape(S, NT)
    harmonic_rows = panel_harmonic[:, pivot]
    delta_x = harmonic_rows[0][:, None] - trail_harmonic[0][None, :] + (ORDERS - 1)
    delta_y = harmonic_rows[1][:, None] - trail_harmonic[1][None, :] + (ORDERS - 1)
    cell_index = (delta_x * DPITCH + delta_y).astype(jnp.int32).reshape(-1)
    gradient = jax.ops.segment_sum(correlation.reshape(-1), cell_index, num_segments=NDIAG)
    eps_grad = gradient * jnp.float32(1.0 / math.sqrt(S * NB))
    return (panel_adjoint, trail_update, eps_grad)
```

```python
import functools
import math

import jax
import jax.numpy as jnp
from jax import lax
from jax.experimental import pallas as pl
from jax.experimental.pallas import tpu as pltpu
from jax.sharding import PartitionSpec as P

NB = 128
S = 18432
ORDERS = 91
DPITCH = 192
NDIAG = 36864
LANES = 128
QUADS = (ORDERS + 3) // 4
XROWS = 4 * QUADS
ACCS = 8
BF = jnp.bfloat16
F32 = jnp.float32

FIRST = (((0,), (0,)), ((), ()))
WHOLE = pl.BlockSpec(memory_space=pltpu.VMEM)
SCALARS = pl.BlockSpec(memory_space=pltpu.SMEM)
ANYWHERE = pl.BlockSpec(memory_space=pl.ANY)


def bits_of(size):
    return [b for b in range(size.bit_length() - 1)]


def swap(x, axis, bit):
    size = lax.axis_size(axis)
    return lax.ppermute(x, axis, [(i, i ^ (1 << bit)) for i in range(size)])


def tile_of(size, options):
    return next(t for t in options if size % t == 0)


def correlate_kernel(chunk, inverse_ref, rhs_ref, field_ref, adjoint_ref, corr_ref, held, sem):
    count = rhs_ref.shape[1] // chunk
    copies = []
    for i in range(count):
        rows = pl.ds(i * chunk, chunk)
        copies.append(pltpu.make_async_copy(field_ref.at[rows], held.at[rows], sem.at[i]))
    for copy in copies:
        copy.start()
    for i in range(count):
        part = slice(i * chunk, (i + 1) * chunk)
        solved = lax.dot_general(
            inverse_ref[...], rhs_ref[:, part], FIRST, preferred_element_type=F32
        )
        adjoint_ref[:, part] = solved.astype(BF)
    for i in range(count):
        copies[i].wait()
        part = slice(i * chunk, (i + 1) * chunk)
        term = jnp.dot(adjoint_ref[:, part], held[part, :], preferred_element_type=F32)
        if i == 0:
            corr_ref[...] = term
        else:
            corr_ref[...] += term


def correlate(inverse, rhs, field):
    sources, cols = field.shape
    chunk = tile_of(sources, (256, 128))
    return pl.pallas_call(
        functools.partial(correlate_kernel, chunk),
        in_specs=[WHOLE, WHOLE, ANYWHERE],
        out_specs=[WHOLE, WHOLE],
        out_shape=[
            jax.ShapeDtypeStruct((NB, sources), BF),
            jax.ShapeDtypeStruct((NB, cols), F32),
        ],
        scratch_shapes=[
            pltpu.VMEM((sources, cols), BF),
            pltpu.SemaphoreType.DMA((sources // chunk,)),
        ],
        name="correlate",
    )(inverse, rhs, field)


def cells_kernel(pivot_ref, panel_ref, corr_ref, odd_ref, slot_ref, out_ref, left, grid, acc):
    corr = corr_ref[...]
    odd = odd_ref[...]
    left[0:NB, :] = jnp.where(odd == 0, corr, 0.0).astype(BF)
    left[NB : 2 * NB, :] = jnp.where(odd == 1, corr, 0.0).astype(BF)
    one, zero = jnp.ones((), BF), jnp.zeros((), BF)

    @pl.loop(0, QUADS)
    def _(n):
        slot = slot_ref[...]
        hot = [
            jnp.where(slot == (2 * n + h).astype(F32).astype(BF), one, zero) for h in range(2)
        ]
        placed = jnp.dot(left[...], jnp.concatenate(hot, axis=1), preferred_element_type=F32)
        for h in range(2):
            for g in range(2):
                grid[pl.ds((4 * n + 2 * h + g) * NB, NB), :] = placed[
                    g * NB : (g + 1) * NB, h * LANES : (h + 1) * LANES
                ]

    acc[...] = jnp.zeros_like(acc)
    lane = lax.broadcasted_iota(jnp.int32, (XROWS, LANES), 1)

    @pl.loop(0, NB // ACCS)
    def _(block):
        for u in range(ACCS):
            a = block * ACCS + u
            row = pivot_ref[a]
            hx, hy = panel_ref[0, row], panel_ref[1, row]
            patch = pltpu.roll(grid[pl.ds(a, XROWS, stride=NB), :], hy, axis=1)
            rows = pl.ds(hx, XROWS)
            acc[2 * u, rows, :] += jnp.where(lane >= hy, patch, 0.0)
            acc[2 * u + 1, rows, :] += jnp.where(lane < hy, patch, 0.0)

    for side in range(2):
        total = acc[side, :DPITCH, :]
        for u in range(1, ACCS):
            total = total + acc[2 * u + side, :DPITCH, :]
        out_ref[:, side * LANES : (side + 1) * LANES] = total


def cells(corr, pivot, panel_harmonic, odd, slot):
    cols = corr.shape[1]
    return pl.pallas_call(
        cells_kernel,
        in_specs=[SCALARS, SCALARS, WHOLE, WHOLE, WHOLE],
        out_specs=WHOLE,
        out_shape=jax.ShapeDtypeStruct((DPITCH, 2 * LANES), F32),
        scratch_shapes=[
            pltpu.VMEM((2 * NB, cols), BF),
            pltpu.VMEM((XROWS * NB, LANES), F32),
            pltpu.VMEM((2 * ACCS, DPITCH + 8, LANES), F32),
        ],
        name="cells",
    )(pivot, panel_harmonic, corr, odd, slot)


def update_kernel(adjoint_ref, factor_ref, trail_ref, *refs):
    out_ref = refs[-1]
    update = lax.dot_general(
        adjoint_ref[...], factor_ref[...], FIRST, preferred_element_type=F32
    )
    out_ref[...] = (trail_ref[...].astype(F32) - update).astype(BF)


def update_part(adjoint, factor, trail, before, tile, first, count):
    sources, cols = trail.shape
    wide = pl.BlockSpec((tile, cols), lambda i: (first + i, 0))
    specs = [
        pl.BlockSpec((NB, tile), lambda i: (0, first + i)),
        pl.BlockSpec((NB, cols), lambda i: (0, 0)),
        wide,
    ]
    operands = [adjoint, factor, trail]
    aliases = {}
    if before is not None:
        specs.append(ANYWHERE)
        operands.append(before)
        aliases = {3: 0}
    rows = tile * count
    return pl.pallas_call(
        update_kernel,
        grid=(count,),
        in_specs=specs,
        out_specs=wide,
        out_shape=jax.ShapeDtypeStruct((sources, cols), BF),
        input_output_aliases=aliases,
        cost_estimate=pl.CostEstimate(
            flops=2 * rows * cols * NB, bytes_accessed=4 * rows * cols, transcendentals=0
        ),
        name="update",
    )(*operands)


def per_device(
    panel_factor,
    diag_inverse,
    panel_rhs,
    trail_rhs,
    forward_field,
    pivot,
    panel_harmonic,
    trail_harmonic,
):
    cols_n, rows_n = lax.axis_size("col"), lax.axis_size("row")
    col, row = lax.axis_index("col"), lax.axis_index("row")

    mirror = (ORDERS - 1) - trail_harmonic
    odd = (mirror[0] % 2)[None, :]
    slot = jnp.where(
        mirror[1][:, None] == jnp.arange(LANES)[None, :], (mirror[0] // 2)[:, None], -1
    ).astype(BF)

    packed = jnp.concatenate([diag_inverse, panel_rhs], axis=1)
    for bit in reversed(bits_of(cols_n)):
        packed = jnp.concatenate([packed, swap(packed, "col", bit)], axis=0)
    inverse, rhs = packed[:, :NB], packed[:, NB:]

    factor = panel_factor
    for bit in bits_of(rows_n):
        factor = jnp.concatenate([factor, swap(factor, "row", bit)], axis=0)
    part = panel_factor.shape[0]
    factor = jnp.concatenate(
        [lax.dynamic_slice_in_dim(factor, (j ^ row) * part, part, 0) for j in range(rows_n)],
        axis=0,
    )

    adjoint, corr = correlate(inverse, rhs, forward_field)
    grad = cells(corr, pivot, panel_harmonic, odd, slot)

    tile = tile_of(trail_rhs.shape[0], (384, 128))
    tiles = trail_rhs.shape[0] // tile
    pieces = 4
    bounds = [tiles * k // pieces for k in range(pieces + 1)]
    trail_update = None
    for lo, hi in zip(bounds[:-1], bounds[1:]):
        if hi > lo:
            trail_update = update_part(
                adjoint, factor, trail_rhs, trail_update, tile, lo, hi - lo
            )

    share = NDIAG // (rows_n * cols_n)
    grad = grad[:, :DPITCH].reshape(rows_n, cols_n, share)
    for bit in bits_of(cols_n):
        mine = (col >> bit) & 1
        pairs = grad.reshape(grad.shape[0], grad.shape[1] // 2, 2, share)
        sent = lax.dynamic_index_in_dim(pairs, 1 - mine, 2, keepdims=False)
        kept = lax.dynamic_index_in_dim(pairs, mine, 2, keepdims=False)
        grad = kept + swap(sent, "col", bit)
    for bit in bits_of(rows_n):
        mine = (row >> bit) & 1
        pairs = grad.reshape(grad.shape[0] // 2, 2, 1, share)
        sent = lax.dynamic_index_in_dim(pairs, 1 - mine, 1, keepdims=False)
        kept = lax.dynamic_index_in_dim(pairs, mine, 1, keepdims=False)
        grad = kept + swap(sent, "row", bit)
    eps_grad = grad.reshape(-1) * jnp.float32(1.0 / math.sqrt(S * NB))
    return (adjoint, trail_update, eps_grad)


def solution(mesh):
    placed = (
        P("row", "col"),
        P("col", None),
        P("col", "row"),
        P("row", "col"),
        P("row", "col"),
        P(),
        P(),
        P(None, "col"),
    )
    return jax.shard_map(
        per_device,
        mesh=mesh,
        in_specs=placed,
        out_specs=(P(None, "row"), P("row", "col"), P(("row", "col"))),
        check_vma=False,
    )
```
